32 devices in a mesh: lon: 4 (over x, core), frame: 8 (over z, y).
Axes of the slice: x: 2, y: 2, z: 4, core: 2. Of those that a mesh axis runs over, the one named last changes fastest.
Arguments:
- layer_input: bfloat16 [8, 16, 512, 128], P('frame', None, 'lon'), may hold values from -6 to 6
- hidden_saved: bfloat16 [8, 16, 512, 128], P('frame', None, 'lon'), as said below
- conv_weight: bfloat16 [3, 3, 128, 128], replicated, may hold values from -0.1875 to 0.1875
- queries: bfloat16 [2048, 128], P('lon'), may hold values from -6 to 6
- corr_cotangent: bfloat16 [8, 49, 2048], P('frame', None, 'lon'), may hold values from -0.59765625 to 0.59765625
- window_rows: int32 [8, 2048], P('frame', 'lon'), may hold values from 0 to 9
- window_cols: int32 [8, 2048], P('frame', 'lon'), may hold values from -3 to 124
- owner_strip: int32 [8, 2048, 1], P('frame', 'lon'), may hold values from 0 to 3; in each aligned block of 512 rows (0 to 511, 512 to 1023, ..., all dimensions but the last counted through in order) at most 128 rows name the same one
Outputs:
- query_grad: float32 [2048, 128], P(('lon', 'frame'))
- first_weight_grad: float32 [3, 3, 128, 128], replicated
- second_weight_grad: float32 [3, 3, 128, 128], replicated
The draws below stay inside these ranges and needn't reach their ends.
Inputs may be any that keep to these rules, and one draw needn't show every extreme that they name: `hidden_saved`: rectifier outputs: zero or positive, a third or more of them exactly zero. `owner_strip`: in each frame, at most 128 of the 512 tracks homed on one strip name the same owning strip.
All inputs are finite; a program needn't handle non-finite values.
Results may differ from the reference program's by a relative error of at most 0.0045.
Values may be sent and summed in bfloat16 or wider, within the bound.
A program may use at most 64 MiB of HBM per device.

```python
import math
import jax
import jax.numpy as jnp
import numpy as np
from jax import lax

C = 128
WIN = 7
ROWS = 16
COLS = 128
TRK_DEV = 512
FRAMES = 8
WIDTH = 512
TRACKS = 2048
CAP = 128
N_LON = 4


def draw_hidden_saved(key, part):
    values = jax.random.normal(key, (FRAMES, ROWS, WIDTH, C), jnp.float32)
    return jnp.maximum(values, 0.0).astype(jnp.bfloat16)


def place_ends(entries, rng, smallest, high):
    longest = entries.shape.index(max(entries.shape))
    spots = []
    for shift in (0, 1):
        where = [jax.random.randint(jax.random.fold_in(rng, axis), (), 0, length) for axis, length in enumerate(entries.shape)]
        where[longest] = (where[longest] + shift) % entries.shape[longest]
        spots.append(tuple(where))
    return entries.at[spots[0]].set(smallest).at[spots[1]].set(high)


def steps_of(rng, shape, cuts, low, largest):
    def one(dim, shards_of):
        steps = jax.random.uniform(jax.random.fold_in(jax.random.fold_in(rng, 6), dim), (shards_of,), jnp.float32, low / len(cuts), largest / len(cuts))
        return jnp.repeat(jnp.exp(steps), shape[dim] // shards_of).reshape((-1,) + (1,) * (len(shape) - dim - 1))

    factor_of = one(*cuts[0])
    for cut in cuts[1:]:
        factor_of = factor_of * one(*cut)
    return factor_of


def shared_out(key, own, number, rows, number_of, top, bound, lean):
    ranking = jax.random.permutation(key, number_of)
    crowded, ordinary = load_shares(number_of, rows * top, bound, lean, True), load_shares(number_of, rows * top, bound, lean, False)
    places = jnp.arange(number_of)

    def named(tallies, turn):
        used = int((tallies > 0).sum())
        fixed = max(1, used // 4)
        passed = fixed + (places - fixed + turn * (used - fixed)) % max(1, number_of - fixed)
        return jnp.zeros((number_of,), jnp.int32).at[ranking[jnp.where(places < fixed, places, passed)]].set(jnp.asarray(tallies, jnp.int32))

    tallies = jnp.where(number % 4 == 0, named(crowded, number // 4), named(ordinary, number - number // 4 - 1))
    mixed = jax.random.permutation(jax.random.fold_in(own, 3), number_of)
    giver, taker = mixed[0:number_of // 2 * 2:2], mixed[1:number_of // 2 * 2:2]
    margin = jnp.minimum(tallies[giver] - 1, bound - tallies[taker]) // 2
    margin = jnp.where((giver == ranking[0]) | (taker == ranking[0]) | (tallies[taker] == 0), 0, jnp.maximum(margin, 0))
    passed = jax.random.randint(jax.random.fold_in(own, 4), (number_of // 2,), 0, 1 << 20) % (margin + 1)
    tallies = tallies.at[giver].add(-passed).at[taker].add(passed)
    labels = jnp.searchsorted(jnp.cumsum(tallies), jnp.arange(rows * top), side="right").astype(jnp.int32)
    table = labels.reshape(top, rows).T
    table = table[jax.random.permutation(jax.random.fold_in(own, 1), rows)]
    turn = jax.random.randint(jax.random.fold_in(own, 2), (rows, 1), 0, top)
    return jnp.take_along_axis(table, (jnp.arange(top)[None, :] + turn) % top, axis=1)


def load_shares(amount, total, limit, lean, full):
    portions = [(1 << 20) // math.isqrt(standing ** lean) + 1 for standing in range(1, amount + 1)]
    largest = limit if full else min(limit, max(-(-total // amount), total * portions[0] // sum(portions)))
    least = 1 if total - largest >= amount - 1 else 0
    counts, surplus = [largest] + [least] * (amount - 1), total - largest - least * (amount - 1)
    while surplus > 0:
        candidates = [i for i in range(1, amount) if counts[i] < largest] or [i for i in range(1, amount) if counts[i] < limit]
        whole, budget = sum([portions[i] for i in candidates]), surplus
        for i in candidates:
            extra = min(limit - counts[i], max(1, budget * portions[i] // whole), surplus)
            counts[i] = counts[i] + extra
            surplus = surplus - extra
    return np.array(counts)


def bell_draw(stream_key, shape, deviation, limit, cuts=(), dtype=jnp.bfloat16):
    gain = steps_of(stream_key, shape, cuts, -0.22, 0.18) if cuts else 1.0
    drawn = jax.random.normal(stream_key, shape, jnp.float32) * deviation * gain
    return jnp.minimum(jnp.maximum(drawn, -limit), limit).astype(dtype)


def setup_inputs(seed: int = 0) -> dict:
    seeds = jax.random.split(jax.random.key(seed), 9)
    layer_input = bell_draw(seeds[0], (FRAMES, ROWS, WIDTH, C), 1.0, 6.0, ((0, 8), (2, 4)))
    hidden_saved = draw_hidden_saved(jax.random.fold_in(seeds[8], 71), 0)
    conv_weight = bell_draw(seeds[2], (3, 3, C, C), (9 * C) ** -0.5, 0.1875)
    queries = bell_draw(seeds[3], (TRACKS, C), 1.0, 6.0, ((0, 4),))
    corr_cotangent = bell_draw(seeds[4], (FRAMES, WIN * WIN, TRACKS), 0.1, 0.59765625, ((0, 8), (2, 4)))
    window_rows = place_ends(jax.random.randint(seeds[5], (FRAMES, TRACKS), 0, ROWS - WIN + 1), jax.random.fold_in(seeds[5], 1), 0, ROWS - WIN).astype(jnp.int32)
    window_cols = place_ends(jax.random.randint(seeds[6], (FRAMES, TRACKS), -3, COLS - 3), jax.random.fold_in(seeds[6], 1), -3, (COLS - 3) - 1).astype(jnp.int32)
    owner_strip_keys = jax.random.split(jax.random.fold_in(seeds[7], 1), FRAMES * TRACKS // TRK_DEV)
    owner_strip_turns = jax.random.permutation(jax.random.fold_in(seeds[7], 3), FRAMES * TRACKS // TRK_DEV)
    owner_strip = jax.vmap(lambda own, number: shared_out(jax.random.fold_in(seeds[7], 2), own, number, TRK_DEV, N_LON, 1, CAP, 2))(owner_strip_keys, owner_strip_turns).reshape((FRAMES, TRACKS, 1))
    return {"layer_input": layer_input, "hidden_saved": hidden_saved, "conv_weight": conv_weight, "queries": queries, "corr_cotangent": corr_cotangent, "window_rows": window_rows, "window_cols": window_cols, "owner_strip": owner_strip}


exact_mode = lax.Precision.HIGHEST

def pad_cells(field):
    padded_rows = jnp.pad(field, ((1, 1), (0, 0), (0, 0)))
    return jnp.concatenate([padded_rows[:, -1:], padded_rows, padded_rows[:, :1]], axis=1)

def forward_conv(padded, weight):
    result = jnp.zeros((ROWS, WIDTH, C), jnp.float32)
    for row_tap in range(3):
        for col_tap in range(3):
            window = padded[row_tap:row_tap + ROWS, col_tap:col_tap + WIDTH]
            result = result + jnp.einsum('rci,io->rco', window, weight[row_tap, col_tap], precision=exact_mode)
    return result

def backward_conv(padded, weight):
    result = jnp.zeros((ROWS, WIDTH, C), jnp.float32)
    for row_tap in range(3):
        for col_tap in range(3):
            window = padded[2 - row_tap:2 - row_tap + ROWS, 2 - col_tap:2 - col_tap + WIDTH]
            result = result + jnp.einsum('rco,io->rci', window, weight[row_tap, col_tap], precision=exact_mode)
    return result

def weight_terms(padded, grad):
    tap_rows = []
    for row_tap in range(3):
        tap_cols = []
        for col_tap in range(3):
            window = padded[row_tap:row_tap + ROWS, col_tap:col_tap + WIDTH]
            tap_cols.append(jnp.einsum('rci,rco->io', window, grad, precision=exact_mode))
        tap_rows.append(jnp.stack(tap_cols))
    return jnp.stack(tap_rows)

def reference(layer_input, hidden_saved, conv_weight, queries, corr_cotangent, window_rows, window_cols, owner_strip):
    weight_full = conv_weight.astype(jnp.float32)
    query_full = queries.astype(jnp.float32)

    def frame_step(carry, frame_items):
        query_acc, first_acc, second_acc = carry
        input_frame, hidden_frame, cotangent, start_rows, start_cols, owners = frame_items
        hidden_padded = pad_cells(hidden_frame.astype(jnp.float32))
        feature = forward_conv(hidden_padded, weight_full).astype(jnp.bfloat16)
        feature = lax.optimization_barrier(feature).astype(jnp.float32)
        base_cols = owners * COLS + start_cols
        feature_grad = jnp.zeros((ROWS, WIDTH, C), jnp.float32)
        query_frame = jnp.zeros((TRACKS, C), jnp.float32)
        for row_off in range(WIN):
            for col_off in range(WIN):
                target_rows = (start_rows + row_off).astype(jnp.int32)
                target_cols = jnp.remainder(base_cols + col_off, WIDTH).astype(jnp.int32)
                weights_here = cotangent[row_off * WIN + col_off].astype(jnp.float32)
                query_frame = query_frame + weights_here[:, None] * feature[target_rows, target_cols]
                feature_grad = feature_grad.at[target_rows, target_cols].add(weights_here[:, None] * query_full)
        grad_rounded = lax.optimization_barrier(feature_grad.astype(jnp.bfloat16)).astype(jnp.float32)
        hidden_grad = backward_conv(pad_cells(grad_rounded), weight_full)
        pre_grad = jnp.where(hidden_frame > 0, hidden_grad, jnp.zeros_like(hidden_grad)).astype(jnp.bfloat16)
        pre_grad = lax.optimization_barrier(pre_grad).astype(jnp.float32)
        second_acc = second_acc + weight_terms(hidden_padded, grad_rounded)
        first_acc = first_acc + weight_terms(pad_cells(input_frame.astype(jnp.float32)), pre_grad)
        return ((query_acc + query_frame, first_acc, second_acc), None)
    start = (jnp.zeros((TRACKS, C), jnp.float32), jnp.zeros((3, 3, C, C), jnp.float32), jnp.zeros((3, 3, C, C), jnp.float32))
    frame_items = (layer_input, hidden_saved, corr_cotangent, window_rows, window_cols, owner_strip[:, :, 0])
    (query_grad, first_sum, second_sum), unused = lax.scan(frame_step, start, frame_items)
    norm_factor = 1.0 / math.sqrt(FRAMES * ROWS * WIDTH)
    return (query_grad, first_sum * norm_factor, second_sum * norm_factor)
```

```python
import functools
import math

import jax
import jax.numpy as jnp
from jax import lax
from jax.experimental import pallas as pl
from jax.experimental.pallas import tpu as pltpu
from jax.sharding import PartitionSpec as P

WIN = 7
WIDE = 144
EXT = 160
BF = jnp.bfloat16
F32 = jnp.float32
MESH = pl.DeviceIdType.MESH
HALO = 9
UNROLL = 32


def dot(a, b):
    return jnp.dot(a, b, preferred_element_type=F32)


def each(count, body):
    if count <= UNROLL:
        for s in range(count):
            body(s)
    else:
        pl.loop(0, count)(body)


def kernel(
    dims,
    x_ref, h_ref, w_ref, q_ref, cot_ref, rows_ref, cols_ref, own_ref,
    query_out, first_out, second_out,
    hext, xext, gext, xh, xx, xg, feat, wb, gt, spread,
    cm, pt, qall, cmall,
    pay_send, pay_recv, strip, halo_send, halo_recv,
    ret_send, ret_recv, retall, qg_send, qg_own, qg_recv,
    grads, half_send, half_recv, acc, rs_send, rs_recv, ag,
    pay_s, pay_r, halo_s, halo_r, ret_s, ret_r, qg_s, qg_r,
    half_s, half_r, rs_s, rs_r, ag_s, ag_r, pair_s, pair_r,
):
    lon_n, frame_n, rows_n, cols_n, chans, tracks, cap, group_n, chunk, scale = dims
    lon, frame = lax.axis_index("lon"), lax.axis_index("frame")
    slots = lon_n * cap
    half = rows_n // 2
    core = lax.rem(lon, 2)
    place = (lon // 2) * frame_n + frame
    part = 9 * chans // 2

    def lon_id(steps):
        return lax.rem(lon + steps + lon_n, lon_n)

    def frame_id(steps):
        return lax.rem(frame + steps + frame_n, frame_n)

    def group_id(steps):
        return lax.rem(place + steps, group_n)

    def group_device(p):
        return {"lon": (p // frame_n) * 2 + core, "frame": lax.rem(p, frame_n)}

    pair = {"lon": lon + 1 - 2 * core}

    def remote(src, dst, send, recv, where):
        return pltpu.make_async_remote_copy(
            src_ref=src, dst_ref=dst, send_sem=send, recv_sem=recv,
            device_id=where, device_id_type=MESH,
        )

    barrier = pltpu.get_barrier_semaphore()
    for step in range(1, lon_n):
        pl.semaphore_signal(barrier, inc=1, device_id={"lon": lon_id(step)}, device_id_type=MESH)

    def greet(s):
        pl.semaphore_signal(
            barrier, inc=1, device_id=group_device(group_id(s + 1)), device_id_type=MESH
        )

    each(group_n - 1, greet)

    for side in range(2):
        edge = cols_n - 8 if side == 0 else 0
        h_edge = h_ref[:, edge : edge + 8].astype(F32)
        x_edge = x_ref[:, edge : edge + 8].astype(F32)
        for r in range(rows_n):
            if side == 0:
                strip[HALO * r : HALO * r + 4, :] = h_edge[r, 4:8]
                strip[HALO * r + 4 : HALO * r + 9, :] = x_edge[r, 3:8]
            else:
                strip[HALO * r : HALO * r + 4, :] = h_edge[r, 0:4]
                strip[HALO * r + 4 : HALO * r + 9, :] = x_edge[r, 0:5]
        halo_send[side] = strip[...].astype(BF)

    owners = own_ref[...]
    marks = (owners == lax.broadcasted_iota(jnp.int32, (16, tracks), 0)).astype(F32)
    earlier = (
        lax.broadcasted_iota(jnp.int32, (tracks, tracks), 0)
        < lax.broadcasted_iota(jnp.int32, (tracks, tracks), 1)
    ).astype(F32).astype(BF)
    before = dot(marks.astype(BF), earlier)
    rank = jnp.sum(before * marks, axis=0, keepdims=True).astype(jnp.int32)
    slot = owners * cap + rank
    cm[...] = jnp.zeros_like(cm)
    for i in range(WIN):
        cm[8 * i : 8 * i + WIN, :] = cot_ref[WIN * i : WIN * i + WIN, :].astype(F32)
    cm[56:57, :] = rows_ref[...].astype(F32)
    cm[57:58, :] = (cols_ref[...] + 3).astype(F32)
    cm_half = cm[...].astype(BF)

    pays = []
    for step in list(range(1, lon_n)) + [0]:
        local = slot - lon_id(step) * cap
        hot = (local == lax.broadcasted_iota(jnp.int32, (cap, tracks), 0)).astype(F32).astype(BF)
        pt[step * cap : (step + 1) * cap, :] = hot
        q_part = dot(hot, q_ref[...]).astype(BF)
        c_part = lax.dot_general(
            cm_half, hot, (((1,), (1,)), ((), ())), preferred_element_type=F32
        )
        if step:
            pay_send[step - 1, 0:cap, :] = q_part
            pay_send[step - 1, cap : cap + 64, :] = c_part.astype(BF)
        else:
            qall[0:cap, :] = q_part
            cmall[:, 0:cap] = c_part

    pl.semaphore_wait(barrier, lon_n - 1 + group_n - 1)
    for step in range(1, lon_n):
        copy = remote(
            pay_send.at[step - 1], pay_recv.at[step - 1], pay_s.at[step - 1],
            pay_r.at[step - 1], {"lon": lon_id(step)},
        )
        copy.start()
        pays.append(copy)
    halos = [
        remote(halo_send.at[0], halo_recv.at[0], halo_s.at[0], halo_r.at[0], {"lon": lon_id(1)}),
        remote(halo_send.at[1], halo_recv.at[1], halo_s.at[1], halo_r.at[1], {"lon": lon_id(-1)}),
    ]
    for copy in halos:
        copy.start()

    for a in range(3):
        for b in range(3):
            tap = w_ref[2 - a, (2 - b) * chans : (3 - b) * chans, :].astype(F32)
            wb[a, b * chans : (b + 1) * chans, :] = tap.T.astype(BF)

    def fill(ext, src):
        ext[...] = jnp.zeros_like(ext)

        @pl.loop(0, rows_n)
        def _(r):
            ext[r + 1, 16 : 16 + cols_n, :] = src[r].astype(F32)

    def side_by_side(ext, out):
        @pl.loop(0, rows_n + 2)
        def _(r):
            for b in range(3):
                out[r, :, b * chans : (b + 1) * chans] = ext[r, 7 + b : 7 + b + WIDE, :].astype(BF)

    def conv(source, weight, r0):
        total = None
        for a in range(3):
            block = source[r0 + a : r0 + a + half].reshape(half * WIDE, 3 * chans)
            term = dot(block, weight[a])
            total = term if total is None else total + term
        return total

    def spread_block(step):
        lanes = slice(step * cap, (step + 1) * cap)
        rows_t = cmall[56:57, lanes].astype(jnp.int32)
        cols_t = cmall[57:58, lanes].astype(jnp.int32) + 5
        placed = []
        for r in range(rows_n):
            value = jnp.zeros((8, cap), F32)
            for i in range(WIN):
                if 0 <= r - i <= rows_n - WIN:
                    value = jnp.where(rows_t == r - i, cmall[8 * i : 8 * i + 8, lanes], value)
            placed.append(value)

        @pl.loop(0, WIDE // 16)
        def _(tile):
            offset = lax.broadcasted_iota(jnp.int32, (16, cap), 0) + tile * 16 - cols_t
            hits = [offset == j for j in range(WIN)]
            for r in range(rows_n):
                value = jnp.zeros((16, cap), F32)
                for j in range(WIN):
                    value = jnp.where(hits[j], placed[r][j : j + 1, :], value)
                start = pl.multiple_of(r * WIDE + tile * 16, 16)
                spread[pl.ds(start, 16), lanes] = value.astype(BF)

    fill(hext, h_ref)
    fill(xext, x_ref)
    gext[...] = jnp.zeros_like(gext)
    spread_block(0)

    for step in range(1, lon_n):
        pays[step - 1].wait()
        qall[step * cap : (step + 1) * cap, :] = pay_recv[step - 1, 0:cap, :]
        cmall[:, step * cap : (step + 1) * cap] = pay_recv[step - 1, cap : cap + 64, :].astype(F32)
        spread_block(step)

    for side in range(2):
        halos[side].wait()
        strip[...] = halo_recv[side].astype(F32)
        for r in range(rows_n):
            h_edge = strip[HALO * r : HALO * r + 4, :]
            x_edge = strip[HALO * r + 4 : HALO * r + 9, :]
            if side == 0:
                hext[r + 1, 12:16, :] = h_edge
                xext[r + 1, 11:16, :] = x_edge
            else:
                hext[r + 1, 16 + cols_n : 20 + cols_n, :] = h_edge
                xext[r + 1, 16 + cols_n : 21 + cols_n, :] = x_edge
    side_by_side(hext, xh)

    for g in range(2):
        cells = slice(g * half * WIDE, (g + 1) * half * WIDE)
        block = dot(spread[cells, :], qall[...])
        gext[1 + g * half : 1 + (g + 1) * half, 8 : 8 + WIDE, :] = block.reshape(half, WIDE, chans)
        gt[:, g * half * WIDE : (g + 1) * half * WIDE] = block.T.astype(BF)

    def halves(which):
        return remote(
            half_send.at[which], half_recv.at[which], half_s.at[which], half_r.at[which], pair
        )

    def scatter(which, s):
        p = group_id(s + 1)
        return remote(
            rs_send.at[which, p], rs_recv.at[which, s], rs_s.at[which, s], rs_r.at[which, s],
            group_device(p),
        )

    def gather(which, s):
        return remote(
            ag.at[which, place], ag.at[which, place], ag_s.at[which, s], ag_r.at[which, s],
            group_device(group_id(s + 1)),
        )

    outs = (second_out, first_out)

    def pairs(which):
        return remote(
            ag.at[which], outs[which].at[core], pair_s.at[which], pair_r.at[which], pair
        )

    def weight_terms(which, source):
        for a in range(3):
            block = source[a : a + rows_n].reshape(rows_n * WIDE, 3 * chans)
            term = dot(gt[...], block) * scale
            for b in range(3):
                row = (3 * a + b) * chans
                grads[which, row : row + chans, :] = term[:, b * chans : (b + 1) * chans].T
        other = pl.ds(pl.multiple_of((1 - core) * part, 8), part)
        half_send[which] = grads[which, other, :].astype(BF)
        halves(which).start()

    def scatter_start(which):
        halves(which).wait()
        mine = pl.ds(pl.multiple_of(core * part, 8), part)
        if group_n * chunk > part:
            acc[part:, :] = jnp.zeros((group_n * chunk - part, chans), F32)
        acc[0:part, :] = grads[which, mine, :] + half_recv[which].astype(F32)
        for p in range(group_n):
            rs_send[which, p] = acc[p * chunk : (p + 1) * chunk, :].astype(BF)
        each(group_n - 1, lambda s: scatter(which, s).start())

    def gather_start(which):
        total = rs_send[which, place].astype(F32)
        if group_n - 1 <= UNROLL:
            for s in range(group_n - 1):
                scatter(which, s).wait()
                total = total + rs_recv[which, s].astype(F32)
        else:
            def add(s, value):
                scatter(which, s).wait()
                return value + rs_recv[which, s].astype(F32)

            total = lax.fori_loop(0, group_n - 1, add, total)
        ag[which, place] = total.astype(BF)
        each(group_n - 1, lambda s: gather(which, s).start())

    def pair_start(which):
        each(group_n - 1, lambda s: gather(which, s).wait())
        pairs(which).start()
        outs[which][core] = ag[which]

    weight_terms(0, xh)

    for g in range(2):
        feat[g * half * WIDE : (g + 1) * half * WIDE, :] = conv(xh, w_ref, g * half).astype(BF)
    slot_grads = lax.dot_general(
        feat[...], spread[...], (((0,), (0,)), ((), ())), preferred_element_type=F32
    )
    retall[:, 0:cap] = slot_grads[:, 0:cap].astype(BF)
    returns = []
    for step in range(1, lon_n):
        ret_send[step - 1] = slot_grads[:, step * cap : (step + 1) * cap].astype(BF)
        copy = remote(
            ret_send.at[step - 1], ret_recv.at[step - 1], ret_s.at[step - 1],
            ret_r.at[step - 1], {"lon": lon_id(-step)},
        )
        copy.start()
        returns.append(copy)

    scatter_start(0)
    side_by_side(gext, xg)
    side_by_side(xext, xx)
    for g in range(2):
        back = conv(xg, wb, g * half).reshape(half, WIDE, chans)
        active = hext[1 + g * half : 1 + (g + 1) * half, 8 : 8 + WIDE, :] > 0
        block = jnp.where(active, back, 0.0).reshape(half * WIDE, chans)
        gt[:, g * half * WIDE : (g + 1) * half * WIDE] = block.T.astype(BF)
    weight_terms(1, xx)

    scatter_start(1)
    for step in range(1, lon_n):
        returns[step - 1].wait()
        retall[:, step * cap : (step + 1) * cap] = ret_recv[step - 1]
    home = dot(retall[...], pt[...]).T
    share = tracks // frame_n
    for f in range(frame_n):
        piece = home[f * share : (f + 1) * share, :]
        qg_own[f] = piece
        qg_send[f] = piece.astype(BF)
    qgs = []
    for step in range(1, frame_n):
        copy = remote(
            qg_send.at[frame_id(step)], qg_recv.at[step - 1], qg_s.at[step - 1],
            qg_r.at[step - 1], {"frame": frame_id(step)},
        )
        copy.start()
        qgs.append(copy)

    gather_start(0)
    gather_start(1)
    pair_start(0)
    total = qg_own[frame]
    for step in range(1, frame_n):
        qgs[step - 1].wait()
        total = total + qg_recv[step - 1].astype(F32)
    query_out[...] = total
    pair_start(1)
    pairs(0).wait()
    pairs(1).wait()


def expand(dims, query_ref, first_ref, second_ref, query_out, first_out, second_out):
    part, group_n, chunk = dims
    query_out[...] = query_ref[...]
    for source, out in ((first_ref, first_out), (second_ref, second_out)):
        for c in range(2):
            for p in range(group_n):
                rows = min(chunk, part - p * chunk)
                if rows > 0:
                    start = c * part + p * chunk
                    out[start : start + rows, :] = source[c, p].astype(F32)[0:rows]


def per_device(
    layer_input, hidden_saved, conv_weight, queries, corr_cotangent,
    window_rows, window_cols, owner_strip,
):
    lon_n, frame_n = lax.axis_size("lon"), lax.axis_size("frame")
    _, rows_n, cols_n, chans = hidden_saved.shape
    tracks = queries.shape[0]
    cap = tracks // 4
    slots = lon_n * cap
    part = 9 * chans // 2
    group_n = lon_n // 2 * frame_n
    chunk = -(-part // group_n)
    scale = 1.0 / math.sqrt(rows_n * cols_n * lon_n * frame_n)
    dims = (lon_n, frame_n, rows_n, cols_n, chans, tracks, cap, group_n, chunk, scale)
    share = tracks // frame_n
    vm = pltpu.VMEM
    dma = pltpu.SemaphoreType.DMA
    scratch = [
        vm((rows_n + 2, EXT, chans), F32),
        vm((rows_n + 2, EXT, chans), F32),
        vm((rows_n + 2, EXT, chans), F32),
        vm((rows_n + 2, WIDE, 3 * chans), BF),
        vm((rows_n + 2, WIDE, 3 * chans), BF),
        vm((rows_n + 2, WIDE, 3 * chans), BF),
        vm((rows_n * WIDE, chans), BF),
        vm((3, 3 * chans, chans), BF),
        vm((chans, rows_n * WIDE), BF),
        vm((rows_n * WIDE, slots), BF),
        vm((64, tracks), F32),
        vm((slots, tracks), BF),
        vm((slots, chans), BF),
        vm((64, slots), F32),
        vm((lon_n - 1, cap + 64, chans), BF),
        vm((lon_n - 1, cap + 64, chans), BF),
        vm((HALO * rows_n, chans), F32),
        vm((2, HALO * rows_n, chans), BF),
        vm((2, HALO * rows_n, chans), BF),
        vm((lon_n - 1, chans, cap), BF),
        vm((lon_n - 1, chans, cap), BF),
        vm((chans, slots), BF),
        vm((frame_n, share, chans), BF),
        vm((frame_n, share, chans), F32),
        vm((frame_n - 1, share, chans), BF),
        vm((2, 9 * chans, chans), F32),
        vm((2, part, chans), BF),
        vm((2, part, chans), BF),
        vm((group_n * chunk, chans), F32),
        vm((2, group_n, chunk, chans), BF),
        vm((2, group_n - 1, chunk, chans), BF),
        vm((2, group_n, chunk, chans), BF),
        dma((lon_n - 1,)), dma((lon_n - 1,)),
        dma((2,)), dma((2,)),
        dma((lon_n - 1,)), dma((lon_n - 1,)),
        dma((frame_n - 1,)), dma((frame_n - 1,)),
        dma((2,)), dma((2,)),
        dma((2, group_n - 1)), dma((2, group_n - 1)),
        dma((2, group_n - 1)), dma((2, group_n - 1)),
        dma((2,)), dma((2,)),
    ]
    spec = pl.BlockSpec(memory_space=pltpu.VMEM)
    gathered = jax.ShapeDtypeStruct((2, group_n, chunk, chans), BF)
    query_grad, first, second = pl.pallas_call(
        functools.partial(kernel, dims),
        out_shape=(jax.ShapeDtypeStruct((share, chans), F32), gathered, gathered),
        in_specs=[spec] * 8,
        out_specs=(spec,) * 3,
        scratch_shapes=scratch,
        compiler_params=pltpu.CompilerParams(
            collective_id=0, has_side_effects=True, vmem_limit_bytes=60 * 1024 * 1024
        ),
    )(
        layer_input[0], hidden_saved[0], conv_weight.reshape(3, 3 * chans, chans), queries,
        corr_cotangent[0], window_rows, window_cols, owner_strip[:, :, 0],
    )
    weight = jax.ShapeDtypeStruct((9 * chans, chans), F32)
    query_grad, first, second = pl.pallas_call(
        functools.partial(expand, (part, group_n, chunk)),
        out_shape=(jax.ShapeDtypeStruct((share, chans), F32), weight, weight),
        in_specs=[spec] * 3,
        out_specs=(spec,) * 3,
    )(query_grad, first, second)
    return (
        query_grad,
        first.reshape(3, 3, chans, chans),
        second.reshape(3, 3, chans, chans),
    )


def solution(mesh):
    placed = (
        P("frame", None, "lon", None),
        P("frame", None, "lon", None),
        P(),
        P("lon", None),
        P("frame", None, "lon"),
        P("frame", "lon"),
        P("frame", "lon"),
        P("frame", "lon", None),
    )
    return jax.shard_map(
        per_device,
        mesh=mesh,
        in_specs=placed,
        out_specs=(P(("lon", "frame"), None), P(), P()),
        check_vma=False,
    )
```

```python
import functools
import math

import jax
import jax.numpy as jnp
from jax import lax
from jax.experimental import pallas as pl
from jax.experimental.pallas import tpu as pltpu
from jax.sharding import PartitionSpec as P

WIN = 7
EDGE = 16
EXT = 160
BF = jnp.bfloat16
F32 = jnp.float32
MESH = pl.DeviceIdType.MESH
HALO = 9
BAND = 4
UNROLL = 32


def dot(a, b):
    return jnp.dot(a, b, preferred_element_type=F32)


def each(count, body):
    if count <= UNROLL:
        for s in range(count):
            body(s)
    else:
        pl.loop(0, count)(body)


def kernel(
    dims,
    x_ref, h_ref, w_ref, q_ref, cot_ref, rows_ref, cols_ref, own_ref,
    query_out, first_out, second_out,
    hext, gext, pext, xh, xhm, xg, xgm, xp, xpm, feat_t, wb, ht, xt, spread, edge,
    cm, pt, qall, cmall,
    pay_send, pay_recv, strip, halo_send, halo_recv,
    ret_send, ret_recv, retall, qg_send, qg_own, qg_recv,
    grads, half_send, half_recv, acc, rs_send, rs_recv, ag,
    pay_s, pay_r, halo_s, halo_r, ret_s, ret_r, qg_s, qg_r,
    half_s, half_r, rs_s, rs_r, ag_s, ag_r, pair_s, pair_r,
):
    lon_n, frame_n, rows_n, cols_n, chans, tracks, cap, group_n, chunk, scale = dims
    lon, frame = lax.axis_index("lon"), lax.axis_index("frame")
    slots = lon_n * cap
    half = rows_n // 2
    core = lax.rem(lon, 2)
    place = (lon // 2) * frame_n + frame
    part = 9 * chans // 2

    def lon_id(steps):
        return lax.rem(lon + steps + lon_n, lon_n)

    def frame_id(steps):
        return lax.rem(frame + steps + frame_n, frame_n)

    def group_id(steps):
        return lax.rem(place + steps, group_n)

    def group_device(p):
        return {"lon": (p // frame_n) * 2 + core, "frame": lax.rem(p, frame_n)}

    pair = {"lon": lon + 1 - 2 * core}

    def remote(src, dst, send, recv, where):
        return pltpu.make_async_remote_copy(
            src_ref=src, dst_ref=dst, send_sem=send, recv_sem=recv,
            device_id=where, device_id_type=MESH,
        )

    barrier = pltpu.get_barrier_semaphore()
    for step in range(1, lon_n):
        pl.semaphore_signal(barrier, inc=1, device_id={"lon": lon_id(step)}, device_id_type=MESH)

    def greet(s):
        pl.semaphore_signal(
            barrier, inc=1, device_id=group_device(group_id(s + 1)), device_id_type=MESH
        )

    each(group_n - 1, greet)

    for side in range(2):
        first = cols_n - 8 if side == 0 else 0
        h_edge = h_ref[:, first : first + 8].astype(F32)
        x_edge = x_ref[:, first : first + 8].astype(F32)
        for r in range(rows_n):
            if side == 0:
                strip[HALO * r : HALO * r + 4, :] = h_edge[r, 4:8]
                strip[HALO * r + 4 : HALO * r + 9, :] = x_edge[r, 3:8]
            else:
                strip[HALO * r : HALO * r + 4, :] = h_edge[r, 0:4]
                strip[HALO * r + 4 : HALO * r + 9, :] = x_edge[r, 0:5]
        halo_send[side] = strip[...].astype(BF)

    owners = own_ref[...]
    marks = (owners == lax.broadcasted_iota(jnp.int32, (16, tracks), 0)).astype(F32)
    earlier = (
        lax.broadcasted_iota(jnp.int32, (tracks, tracks), 0)
        < lax.broadcasted_iota(jnp.int32, (tracks, tracks), 1)
    ).astype(F32).astype(BF)
    before = dot(marks.astype(BF), earlier)
    rank = jnp.sum(before * marks, axis=0, keepdims=True).astype(jnp.int32)
    slot = owners * cap + rank
    cm[...] = jnp.zeros_like(cm)
    for i in range(WIN):
        cm[8 * i : 8 * i + WIN, :] = cot_ref[WIN * i : WIN * i + WIN, :].astype(F32)
    cm[56:57, :] = rows_ref[...].astype(F32)
    cm[57:58, :] = (cols_ref[...] + 3).astype(F32)
    cm_half = cm[...].astype(BF)

    pays = []
    for step in list(range(1, lon_n)) + [0]:
        local = slot - lon_id(step) * cap
        hot = (local == lax.broadcasted_iota(jnp.int32, (cap, tracks), 0)).astype(F32).astype(BF)
        pt[step * cap : (step + 1) * cap, :] = hot
        q_part = dot(hot, q_ref[...]).astype(BF)
        c_part = lax.dot_general(
            cm_half, hot, (((1,), (1,)), ((), ())), preferred_element_type=F32
        )
        if step:
            pay_send[step - 1, 0:cap, :] = q_part
            pay_send[step - 1, cap : cap + 64, :] = c_part.astype(BF)
        else:
            qall[0:cap, :] = q_part
            cmall[:, 0:cap] = c_part

    pl.semaphore_wait(barrier, lon_n - 1 + group_n - 1)
    for step in range(1, lon_n):
        copy = remote(
            pay_send.at[step - 1], pay_recv.at[step - 1], pay_s.at[step - 1],
            pay_r.at[step - 1], {"lon": lon_id(step)},
        )
        copy.start()
        pays.append(copy)
    halos = [
        remote(halo_send.at[0], halo_recv.at[0], halo_s.at[0], halo_r.at[0], {"lon": lon_id(1)}),
        remote(halo_send.at[1], halo_recv.at[1], halo_s.at[1], halo_r.at[1], {"lon": lon_id(-1)}),
    ]
    for copy in halos:
        copy.start()

    for a in range(3):
        for b in range(3):
            tap = w_ref[2 - a, b * chans : (b + 1) * chans, :].astype(F32)
            wb[a, b * chans : (b + 1) * chans, :] = tap.T.astype(BF)

    cells, rim = rows_n * cols_n, rows_n * EDGE

    def turned(src, out):
        out[0:chans, 0:cols_n] = jnp.zeros((chans, cols_n), BF)
        out[2 * chans : 3 * chans, cells - cols_n : cells] = jnp.zeros((chans, cols_n), BF)
        for r in range(rows_n):
            tile = src[r].astype(F32).T.astype(BF)
            for a in range(3):
                if 0 <= r + 1 - a < rows_n:
                    at = (r + 1 - a) * cols_n
                    out[a * chans : (a + 1) * chans, at : at + cols_n] = tile

    def turned_edge(out):
        for a in range(3):
            block = edge[a : a + rows_n].reshape(rim, chans)
            out[a * chans : (a + 1) * chans, cells : cells + rim] = block.T.astype(BF)

    def side_by_side(ext, out, out_edge, flip):
        for r in range(1, rows_n + 1):
            at, low = r * cols_n, r * EDGE
            for b in range(3):
                by = 1 - b if flip else b - 1
                lanes = slice(b * chans, (b + 1) * chans)
                out[pl.ds(at, cols_n), lanes] = ext[r, 16 + by : 16 + by + cols_n, :].astype(BF)
                rim_cells = jnp.concatenate(
                    [
                        ext[r, 8 + by : 16 + by, :],
                        ext[r, 16 + cols_n + by : 24 + cols_n + by, :],
                    ],
                    axis=0,
                )
                out_edge[pl.ds(low, EDGE), lanes] = rim_cells.astype(BF)

    def conv(source, weight, start, count, step):
        total = None
        for a in range(3):
            term = dot(source[pl.ds(start + a * step, count), :], weight[a])
            total = term if total is None else total + term
        return total

    def spread_block(step):
        lanes = slice(step * cap, (step + 1) * cap)
        rows_t = cmall[56:57, lanes].astype(jnp.int32)
        cols_t = cmall[57:58, lanes].astype(jnp.int32) - 3
        placed = []
        for r in range(rows_n):
            value = jnp.zeros((8, cap), F32)
            for i in range(WIN):
                if 0 <= r - i <= rows_n - WIN:
                    value = jnp.where(rows_t == r - i, cmall[8 * i : 8 * i + 8, lanes], value)
            placed.append(value)

        def tiles(column, base, stride):
            offset = column - cols_t
            hits = [offset == j for j in range(WIN)]
            for r in range(rows_n):
                value = jnp.zeros((16, cap), F32)
                for j in range(WIN):
                    value = jnp.where(hits[j], placed[r][j : j + 1, :], value)
                start = pl.multiple_of(r * stride + base, 16)
                spread[pl.ds(start, 16), lanes] = value.astype(BF)

        count = lax.broadcasted_iota(jnp.int32, (16, cap), 0)

        @pl.loop(0, cols_n // 16)
        def _(tile):
            tiles(count + tile * 16, tile * 16, cols_n)

        tiles(jnp.where(count < 8, count - 8, count + (cols_n - 8)), cells, EDGE)

    hext[...] = jnp.zeros_like(hext)
    gext[...] = jnp.zeros_like(gext)
    pext[...] = jnp.zeros_like(pext)

    @pl.loop(0, rows_n)
    def _(r):
        hext[r + 1, 16 : 16 + cols_n, :] = h_ref[r].astype(F32)

    for wide in (xh, xg, xp):
        wide[0:cols_n, :] = jnp.zeros((cols_n, 3 * chans), BF)
        wide[cells + cols_n :, :] = jnp.zeros((cols_n, 3 * chans), BF)
    for thin in (xhm, xgm, xpm):
        thin[0:EDGE, :] = jnp.zeros((EDGE, 3 * chans), BF)
        thin[rim + EDGE :, :] = jnp.zeros((EDGE, 3 * chans), BF)

    turned(h_ref, ht)
    turned(x_ref, xt)
    spread_block(0)

    for step in range(1, lon_n):
        pays[step - 1].wait()
        qall[step * cap : (step + 1) * cap, :] = pay_recv[step - 1, 0:cap, :]
        cmall[:, step * cap : (step + 1) * cap] = pay_recv[step - 1, cap : cap + 64, :].astype(F32)
        spread_block(step)

    def to_rim(ext, block):
        block = block.reshape(rows_n, EDGE, chans)
        ext[1 : 1 + rows_n, 8:16, :] = block[:, 0:8]
        ext[1 : 1 + rows_n, 16 + cols_n : 24 + cols_n, :] = block[:, 8:16]

    for g in range(rows_n // BAND):
        low = g * BAND * cols_n
        block = dot(spread[pl.ds(low, BAND * cols_n), :], qall[...])
        gext[pl.ds(1 + g * BAND, BAND), 16 : 16 + cols_n, :] = block.reshape(BAND, cols_n, chans)

    to_rim(gext, dot(spread[cells : cells + rim, :], qall[...]))
    for copy in halos:
        copy.wait()

    def unpack(side, first, count, out_at, in_edge):
        strip[...] = halo_recv[side].astype(F32)
        for r in range(rows_n):
            at = HALO * r + first
            edge[r + 1, in_edge : in_edge + count, :] = strip[at : at + count, :]
            if out_at:
                hext[r + 1, out_at : out_at + count, :] = strip[at : at + count, :]

    edge[...] = jnp.zeros_like(edge)
    unpack(0, 0, 4, 12, 4)
    unpack(1, 0, 4, 16 + cols_n, 8)
    turned_edge(ht)
    side_by_side(gext, xg, xgm, True)

    def halves(which):
        return remote(
            half_send.at[which], half_recv.at[which], half_s.at[which], half_r.at[which], pair
        )

    def scatter(which, s):
        p = group_id(s + 1)
        return remote(
            rs_send.at[which, p], rs_recv.at[which, s], rs_s.at[which, s], rs_r.at[which, s],
            group_device(p),
        )

    def gather(which, s):
        return remote(
            ag.at[which, place], ag.at[which, place], ag_s.at[which, s], ag_r.at[which, s],
            group_device(group_id(s + 1)),
        )

    outs = (second_out, first_out)

    def pairs(which):
        return remote(
            ag.at[which], outs[which].at[core], pair_s.at[which], pair_r.at[which], pair
        )

    def weight_terms(which, turned_source, grad, grad_edge):
        term = dot(turned_source[:, 0:cells], grad[cols_n : cols_n + cells, :])
        term = term + dot(turned_source[:, cells : cells + rim], grad_edge[EDGE : EDGE + rim, :])
        term = term * scale
        for a in range(3):
            for b in range(3):
                row = (3 * a + b) * chans
                grads[which, row : row + chans, :] = term[
                    a * chans : (a + 1) * chans, b * chans : (b + 1) * chans
                ]
        other = pl.ds(pl.multiple_of((1 - core) * part, 8), part)
        half_send[which] = grads[which, other, :].astype(BF)
        halves(which).start()

    def scatter_start(which):
        halves(which).wait()
        mine = pl.ds(pl.multiple_of(core * part, 8), part)
        if group_n * chunk > part:
            acc[part:, :] = jnp.zeros((group_n * chunk - part, chans), F32)
        acc[0:part, :] = grads[which, mine, :] + half_recv[which].astype(F32)
        for p in range(group_n):
            rs_send[which, p] = acc[p * chunk : (p + 1) * chunk, :].astype(BF)
        each(group_n - 1, lambda s: scatter(which, s).start())

    def gather_start(which):
        total = rs_send[which, place].astype(F32)
        if group_n - 1 <= UNROLL:
            for s in range(group_n - 1):
                scatter(which, s).wait()
                total = total + rs_recv[which, s].astype(F32)
        else:
            def add(s, value):
                scatter(which, s).wait()
                return value + rs_recv[which, s].astype(F32)

            total = lax.fori_loop(0, group_n - 1, add, total)
        ag[which, place] = total.astype(BF)
        each(group_n - 1, lambda s: gather(which, s).start())

    def pair_start(which):
        each(group_n - 1, lambda s: gather(which, s).wait())
        pairs(which).start()
        outs[which][core] = ag[which]

    weight_terms(0, ht, xg, xgm)

    edge[...] = jnp.zeros_like(edge)
    unpack(0, 4, 5, 0, 3)
    unpack(1, 4, 5, 0, 8)
    turned_edge(xt)

    side_by_side(hext, xh, xhm, False)
    for g in range(rows_n // BAND):
        low = g * BAND * cols_n
        block = conv(xh, w_ref, low, BAND * cols_n, cols_n)
        feat_t[:, pl.ds(low, BAND * cols_n)] = block.T.astype(BF)

    feat_t[:, cells : cells + rim] = conv(xhm, w_ref, 0, rim, EDGE).T.astype(BF)

    scatter_start(0)
    slot_grads = dot(feat_t[...], spread[...])
    retall[:, 0:cap] = slot_grads[:, 0:cap].astype(BF)
    returns = []
    for step in range(1, lon_n):
        ret_send[step - 1] = slot_grads[:, step * cap : (step + 1) * cap].astype(BF)
        copy = remote(
            ret_send.at[step - 1], ret_recv.at[step - 1], ret_s.at[step - 1],
            ret_r.at[step - 1], {"lon": lon_id(-step)},
        )
        copy.start()
        returns.append(copy)

    for g in range(rows_n // BAND):
        low = g * BAND * cols_n
        back = conv(xg, wb, low, BAND * cols_n, cols_n).reshape(BAND, cols_n, chans)
        rows = pl.ds(1 + g * BAND, BAND)
        active = hext[rows, 16 : 16 + cols_n, :] > 0
        pext[rows, 16 : 16 + cols_n, :] = jnp.where(active, back, 0.0)

    rim_active = jnp.concatenate(
        [hext[1 : 1 + rows_n, 8:16, :], hext[1 : 1 + rows_n, 16 + cols_n : 24 + cols_n, :]],
        axis=1,
    ).reshape(rim, chans) > 0
    to_rim(pext, jnp.where(rim_active, conv(xgm, wb, 0, rim, EDGE), 0.0))
    side_by_side(pext, xp, xpm, True)
    weight_terms(1, xt, xp, xpm)

    scatter_start(1)
    gather_start(0)
    gather_start(1)
    for step in range(1, lon_n):
        returns[step - 1].wait()
        retall[:, step * cap : (step + 1) * cap] = ret_recv[step - 1]
    home = dot(retall[...], pt[...]).T
    share = tracks // frame_n
    for f in range(frame_n):
        piece = home[f * share : (f + 1) * share, :]
        qg_own[f] = piece
        qg_send[f] = piece.astype(BF)
    qgs = []
    for step in range(1, frame_n):
        copy = remote(
            qg_send.at[frame_id(step)], qg_recv.at[step - 1], qg_s.at[step - 1],
            qg_r.at[step - 1], {"frame": frame_id(step)},
        )
        copy.start()
        qgs.append(copy)

    pair_start(0)
    pair_start(1)
    total = qg_own[frame]
    for step in range(1, frame_n):
        qgs[step - 1].wait()
        total = total + qg_recv[step - 1].astype(F32)
    query_out[...] = total
    pairs(0).wait()
    pairs(1).wait()


def expand(dims, query_ref, first_ref, second_ref, query_out, first_out, second_out):
    part, group_n, chunk = dims
    query_out[...] = query_ref[...]
    for source, out in ((first_ref, first_out), (second_ref, second_out)):
        for c in range(2):
            for p in range(group_n):
                rows = min(chunk, part - p * chunk)
                if rows > 0:
                    start = c * part + p * chunk
                    out[start : start + rows, :] = source[c, p].astype(F32)[0:rows]


def per_device(
    layer_input, hidden_saved, conv_weight, queries, corr_cotangent,
    window_rows, window_cols, owner_strip,
):
    lon_n, frame_n = lax.axis_size("lon"), lax.axis_size("frame")
    _, rows_n, cols_n, chans = hidden_saved.shape
    tracks = queries.shape[0]
    cap = tracks // 4
    slots = lon_n * cap
    part = 9 * chans // 2
    group_n = lon_n // 2 * frame_n
    chunk = -(-part // group_n)
    scale = 1.0 / math.sqrt(rows_n * cols_n * lon_n * frame_n)
    dims = (lon_n, frame_n, rows_n, cols_n, chans, tracks, cap, group_n, chunk, scale)
    share = tracks // frame_n
    vm = pltpu.VMEM
    dma = pltpu.SemaphoreType.DMA
    scratch = [
        vm((rows_n + 2, EXT, chans), F32),
        vm((rows_n + 2, EXT, chans), F32),
        vm((rows_n + 2, EXT, chans), F32),
        vm(((rows_n + 2) * cols_n, 3 * chans), BF),
        vm(((rows_n + 2) * EDGE, 3 * chans), BF),
        vm(((rows_n + 2) * cols_n, 3 * chans), BF),
        vm(((rows_n + 2) * EDGE, 3 * chans), BF),
        vm(((rows_n + 2) * cols_n, 3 * chans), BF),
        vm(((rows_n + 2) * EDGE, 3 * chans), BF),
        vm((chans, rows_n * (cols_n + EDGE)), BF),
        vm((3, 3 * chans, chans), BF),
        vm((3 * chans, rows_n * (cols_n + EDGE)), BF),
        vm((3 * chans, rows_n * (cols_n + EDGE)), BF),
        vm((rows_n * (cols_n + EDGE), slots), BF),
        vm((rows_n + 2, EDGE, chans), F32),
        vm((64, tracks), F32),
        vm((slots, tracks), BF),
        vm((slots, chans), BF),
        vm((64, slots), F32),
        vm((lon_n - 1, cap + 64, chans), BF),
        vm((lon_n - 1, cap + 64, chans), BF),
        vm((HALO * rows_n, chans), F32),
        vm((2, HALO * rows_n, chans), BF),
        vm((2, HALO * rows_n, chans), BF),
        vm((lon_n - 1, chans, cap), BF),
        vm((lon_n - 1, chans, cap), BF),
        vm((chans, slots), BF),
        vm((frame_n, share, chans), BF),
        vm((frame_n, share, chans), F32),
        vm((frame_n - 1, share, chans), BF),
        vm((2, 9 * chans, chans), F32),
        vm((2, part, chans), BF),
        vm((2, part, chans), BF),
        vm((group_n * chunk, chans), F32),
        vm((2, group_n, chunk, chans), BF),
        vm((2, group_n - 1, chunk, chans), BF),
        vm((2, group_n, chunk, chans), BF),
        dma((lon_n - 1,)), dma((lon_n - 1,)),
        dma((2,)), dma((2,)),
        dma((lon_n - 1,)), dma((lon_n - 1,)),
        dma((frame_n - 1,)), dma((frame_n - 1,)),
        dma((2,)), dma((2,)),
        dma((2, group_n - 1)), dma((2, group_n - 1)),
        dma((2, group_n - 1)), dma((2, group_n - 1)),
        dma((2,)), dma((2,)),
    ]
    spec = pl.BlockSpec(memory_space=pltpu.VMEM)
    gathered = jax.ShapeDtypeStruct((2, group_n, chunk, chans), BF)
    query_grad, first, second = pl.pallas_call(
        functools.partial(kernel, dims),
        out_shape=(jax.ShapeDtypeStruct((share, chans), F32), gathered, gathered),
        in_specs=[spec] * 8,
        out_specs=(spec,) * 3,
        scratch_shapes=scratch,
        compiler_params=pltpu.CompilerParams(
            collective_id=0, has_side_effects=True, vmem_limit_bytes=60 * 1024 * 1024
        ),
    )(
        layer_input[0], hidden_saved[0], conv_weight.reshape(3, 3 * chans, chans), queries,
        corr_cotangent[0], window_rows, window_cols, owner_strip[:, :, 0],
    )
    weight = jax.ShapeDtypeStruct((9 * chans, chans), F32)
    query_grad, first, second = pl.pallas_call(
        functools.partial(expand, (part, group_n, chunk)),
        out_shape=(jax.ShapeDtypeStruct((share, chans), F32), weight, weight),
        in_specs=[spec] * 3,
        out_specs=(spec,) * 3,
    )(query_grad, first, second)
    return (
        query_grad,
        first.reshape(3, 3, chans, chans),
        second.reshape(3, 3, chans, chans),
    )


def solution(mesh):
    placed = (
        P("frame", None, "lon", None),
        P("frame", None, "lon", None),
        P(),
        P("lon", None),
        P("frame", None, "lon"),
        P("frame", "lon"),
        P("frame", "lon"),
        P("frame", "lon", None),
    )
    return jax.shard_map(
        per_device,
        mesh=mesh,
        in_specs=placed,
        out_specs=(P(("lon", "frame"), None), P(), P()),
        check_vma=False,
    )
```

```python
import functools
import math

import jax
import jax.numpy as jnp
from jax import lax
from jax.experimental import pallas as pl
from jax.experimental.pallas import tpu as pltpu
from jax.sharding import PartitionSpec as P

WIN = 7
EDGE = 16
EXT = 160
BF = jnp.bfloat16
F32 = jnp.float32
MESH = pl.DeviceIdType.MESH
HALO = 9
BAND = 4
UNROLL = 32


def dot(a, b):
    return jnp.dot(a, b, preferred_element_type=F32)


def each(count, body):
    if count <= UNROLL:
        for s in range(count):
            body(s)
    else:
        pl.loop(0, count)(body)


def kernel(
    dims,
    x_ref, h_ref, w_ref, q_ref, cot_ref, rows_ref, cols_ref, own_ref,
    query_out, first_out, second_out,
    hext, gext, pext, xh, xhm, xg, xgm, xp, xpm, feat_t, wb, ht, xt, spread, edge,
    cm, pt, qall, cmall,
    pay_send, pay_recv, strip, halo_send, halo_recv,
    ret_send, ret_recv, retall, qg_send, qg_own, qg_recv,
    grads, half_send, half_recv, acc, rs_send, rs_recv, ag,
    pay_s, pay_r, halo_s, halo_r, ret_s, ret_r, qg_s, qg_r,
    half_s, half_r, rs_s, rs_r, ag_s, ag_r, pair_s, pair_r,
):
    lon_n, frame_n, rows_n, cols_n, chans, tracks, cap, group_n, chunk, scale = dims
    lon, frame = lax.axis_index("lon"), lax.axis_index("frame")
    slots = lon_n * cap
    half = rows_n // 2
    core = lax.rem(lon, 2)
    place = (lon // 2) * frame_n + frame
    part = 9 * chans // 2

    def lon_id(steps):
        return lax.rem(lon + steps + lon_n, lon_n)

    def frame_id(steps):
        return lax.rem(frame + steps + frame_n, frame_n)

    def group_id(steps):
        return lax.rem(place + steps, group_n)

    def group_device(p):
        return {"lon": (p // frame_n) * 2 + core, "frame": lax.rem(p, frame_n)}

    pair = {"lon": lon + 1 - 2 * core}

    def remote(src, dst, send, recv, where):
        return pltpu.make_async_remote_copy(
            src_ref=src, dst_ref=dst, send_sem=send, recv_sem=recv,
            device_id=where, device_id_type=MESH,
        )

    barrier = pltpu.get_barrier_semaphore()
    for step in range(1, lon_n):
        pl.semaphore_signal(barrier, inc=1, device_id={"lon": lon_id(step)}, device_id_type=MESH)

    def greet(s):
        pl.semaphore_signal(
            barrier, inc=1, device_id=group_device(group_id(s + 1)), device_id_type=MESH
        )

    each(group_n - 1, greet)

    for side in range(2):
        first = cols_n - 8 if side == 0 else 0
        h_edge = h_ref[:, first : first + 8].astype(F32)
        x_edge = x_ref[:, first : first + 8].astype(F32)
        for r in range(rows_n):
            if side == 0:
                strip[HALO * r : HALO * r + 4, :] = h_edge[r, 4:8]
                strip[HALO * r + 4 : HALO * r + 9, :] = x_edge[r, 3:8]
            else:
                strip[HALO * r : HALO * r + 4, :] = h_edge[r, 0:4]
                strip[HALO * r + 4 : HALO * r + 9, :] = x_edge[r, 0:5]
        halo_send[side] = strip[...].astype(BF)

    owners = own_ref[...]
    marks = (owners == lax.broadcasted_iota(jnp.int32, (16, tracks), 0)).astype(F32)
    earlier = (
        lax.broadcasted_iota(jnp.int32, (tracks, tracks), 0)
        < lax.broadcasted_iota(jnp.int32, (tracks, tracks), 1)
    ).astype(F32).astype(BF)
    before = dot(marks.astype(BF), earlier)
    rank = jnp.sum(before * marks, axis=0, keepdims=True).astype(jnp.int32)
    slot = owners * cap + rank
    cm[...] = jnp.zeros_like(cm)
    for i in range(WIN):
        cm[8 * i : 8 * i + WIN, :] = cot_ref[WIN * i : WIN * i + WIN, :].astype(F32)
    cm[56:57, :] = rows_ref[...].astype(F32)
    cm[57:58, :] = (cols_ref[...] + 3).astype(F32)
    cm_half = cm[...].astype(BF)

    pays = []
    for step in list(range(1, lon_n)) + [0]:
        local = slot - lon_id(step) * cap
        hot = (local == lax.broadcasted_iota(jnp.int32, (cap, tracks), 0)).astype(F32).astype(BF)
        pt[step * cap : (step + 1) * cap, :] = hot
        q_part = dot(hot, q_ref[...]).astype(BF)
        c_part = lax.dot_general(
            cm_half, hot, (((1,), (1,)), ((), ())), preferred_element_type=F32
        )
        if step:
            pay_send[step - 1, 0:cap, :] = q_part
            pay_send[step - 1, cap : cap + 64, :] = c_part.astype(BF)
        else:
            qall[0:cap, :] = q_part
            cmall[:, 0:cap] = c_part

    pl.semaphore_wait(barrier, lon_n - 1 + group_n - 1)
    for step in range(1, lon_n):
        copy = remote(
            pay_send.at[step - 1], pay_recv.at[step - 1], pay_s.at[step - 1],
            pay_r.at[step - 1], {"lon": lon_id(step)},
        )
        copy.start()
        pays.append(copy)
    halos = [
        remote(halo_send.at[0], halo_recv.at[0], halo_s.at[0], halo_r.at[0], {"lon": lon_id(1)}),
        remote(halo_send.at[1], halo_recv.at[1], halo_s.at[1], halo_r.at[1], {"lon": lon_id(-1)}),
    ]
    for copy in halos:
        copy.start()

    for a in range(3):
        for b in range(3):
            tap = w_ref[2 - a, b * chans : (b + 1) * chans, :].astype(F32)
            wb[a, b * chans : (b + 1) * chans, :] = tap.T.astype(BF)

    cells, rim = rows_n * cols_n, rows_n * EDGE

    def turned(src, out):
        out[0:chans, 0:cols_n] = jnp.zeros((chans, cols_n), BF)
        out[2 * chans : 3 * chans, cells - cols_n : cells] = jnp.zeros((chans, cols_n), BF)
        for r in range(rows_n):
            tile = src[r].astype(F32).T.astype(BF)
            for a in range(3):
                if 0 <= r + 1 - a < rows_n:
                    at = (r + 1 - a) * cols_n
                    out[a * chans : (a + 1) * chans, at : at + cols_n] = tile

    def turned_edge(out):
        for a in range(3):
            block = edge[a : a + rows_n].reshape(rim, chans)
            out[a * chans : (a + 1) * chans, cells : cells + rim] = block.T.astype(BF)

    def side_by_side(ext, out, out_edge, flip):
        for r in range(1, rows_n + 1):
            at, low = r * cols_n, r * EDGE
            for b in range(3):
                by = 1 - b if flip else b - 1
                lanes = slice(b * chans, (b + 1) * chans)
                out[pl.ds(at, cols_n), lanes] = ext[r, 16 + by : 16 + by + cols_n, :].astype(BF)
                rim_cells = jnp.concatenate(
                    [
                        ext[r, 8 + by : 16 + by, :],
                        ext[r, 16 + cols_n + by : 24 + cols_n + by, :],
                    ],
                    axis=0,
                )
                out_edge[pl.ds(low, EDGE), lanes] = rim_cells.astype(BF)

    def conv(source, weight, start, count, step):
        total = None
        for a in range(3):
            term = dot(source[pl.ds(start + a * step, count), :], weight[a])
            total = term if total is None else total + term
        return total

    def spread_block(step):
        lanes = slice(step * cap, (step + 1) * cap)
        rows_t = cmall[56:57, lanes].astype(jnp.int32)
        cols_t = cmall[57:58, lanes].astype(jnp.int32) - 3
        placed = []
        for r in range(rows_n):
            value = jnp.zeros((8, cap), F32)
            for i in range(WIN):
                if 0 <= r - i <= rows_n - WIN:
                    value = jnp.where(rows_t == r - i, cmall[8 * i : 8 * i + 8, lanes], value)
            placed.append(value)

        def tiles(column, base, stride):
            offset = column - cols_t
            hits = [offset == j for j in range(WIN)]
            for r in range(rows_n):
                value = jnp.zeros((16, cap), F32)
                for j in range(WIN):
                    value = jnp.where(hits[j], placed[r][j : j + 1, :], value)
                start = pl.multiple_of(r * stride + base, 16)
                spread[pl.ds(start, 16), lanes] = value.astype(BF)

        count = lax.broadcasted_iota(jnp.int32, (16, cap), 0)

        @pl.loop(0, cols_n // 16)
        def _(tile):
            tiles(count + tile * 16, tile * 16, cols_n)

        tiles(jnp.where(count < 8, count - 8, count + (cols_n - 8)), cells, EDGE)

    hext[...] = jnp.zeros_like(hext)
    gext[...] = jnp.zeros_like(gext)
    pext[...] = jnp.zeros_like(pext)

    @pl.loop(0, rows_n)
    def _(r):
        hext[r + 1, 16 : 16 + cols_n, :] = h_ref[r].astype(F32)

    for wide in (xh, xg, xp):
        wide[0:cols_n, :] = jnp.zeros((cols_n, 3 * chans), BF)
        wide[cells + cols_n :, :] = jnp.zeros((cols_n, 3 * chans), BF)
    for thin in (xhm, xgm, xpm):
        thin[0:EDGE, :] = jnp.zeros((EDGE, 3 * chans), BF)
        thin[rim + EDGE :, :] = jnp.zeros((EDGE, 3 * chans), BF)

    turned(h_ref, ht)
    turned(x_ref, xt)
    spread_block(0)

    for step in range(1, lon_n):
        pays[step - 1].wait()
        qall[step * cap : (step + 1) * cap, :] = pay_recv[step - 1, 0:cap, :]
        cmall[:, step * cap : (step + 1) * cap] = pay_recv[step - 1, cap : cap + 64, :].astype(F32)
        spread_block(step)

    def to_rim(ext, block):
        block = block.reshape(rows_n, EDGE, chans)
        ext[1 : 1 + rows_n, 8:16, :] = block[:, 0:8]
        ext[1 : 1 + rows_n, 16 + cols_n : 24 + cols_n, :] = block[:, 8:16]

    for g in range(rows_n // BAND):
        low = g * BAND * cols_n
        block = dot(spread[pl.ds(low, BAND * cols_n), :], qall[...])
        gext[pl.ds(1 + g * BAND, BAND), 16 : 16 + cols_n, :] = block.reshape(BAND, cols_n, chans)

    to_rim(gext, dot(spread[cells : cells + rim, :], qall[...]))
    for copy in halos:
        copy.wait()

    def unpack(side, first, count, out_at, in_edge):
        strip[...] = halo_recv[side].astype(F32)
        for r in range(rows_n):
            at = HALO * r + first
            edge[r + 1, in_edge : in_edge + count, :] = strip[at : at + count, :]
            if out_at:
                hext[r + 1, out_at : out_at + count, :] = strip[at : at + count, :]

    edge[...] = jnp.zeros_like(edge)
    unpack(0, 0, 4, 12, 4)
    unpack(1, 0, 4, 16 + cols_n, 8)
    turned_edge(ht)
    side_by_side(gext, xg, xgm, True)

    def halves(which):
        return remote(
            half_send.at[which], half_recv.at[which], half_s.at[which], half_r.at[which], pair
        )

    def scatter(which, s):
        p = group_id(s + 1)
        return remote(
            rs_send.at[which, p], rs_recv.at[which, s], rs_s.at[which, s], rs_r.at[which, s],
            group_device(p),
        )

    def gather(which, s):
        return remote(
            ag.at[which, place], ag.at[which, place], ag_s.at[which, s], ag_r.at[which, s],
            group_device(group_id(s + 1)),
        )

    outs = (second_out, first_out)

    def pairs(which):
        return remote(
            ag.at[which], outs[which].at[core], pair_s.at[which], pair_r.at[which], pair
        )

    def weight_terms(which, turned_source, grad, grad_edge):
        term = dot(turned_source[:, 0:cells], grad[cols_n : cols_n + cells, :])
        term = term + dot(turned_source[:, cells : cells + rim], grad_edge[EDGE : EDGE + rim, :])
        term = term * scale
        for a in range(3):
            for b in range(3):
                row = (3 * a + b) * chans
                grads[which, row : row + chans, :] = term[
                    a * chans : (a + 1) * chans, b * chans : (b + 1) * chans
                ]
        other = pl.ds(pl.multiple_of((1 - core) * part, 8), part)
        half_send[which] = grads[which, other, :].astype(BF)
        halves(which).start()

    def scatter_start(which):
        halves(which).wait()
        mine = pl.ds(pl.multiple_of(core * part, 8), part)
        if group_n * chunk > part:
            acc[part:, :] = jnp.zeros((group_n * chunk - part, chans), F32)
        acc[0:part, :] = grads[which, mine, :] + half_recv[which].astype(F32)
        for p in range(group_n):
            rs_send[which, p] = acc[p * chunk : (p + 1) * chunk, :].astype(BF)
        each(group_n - 1, lambda s: scatter(which, s).start())

    def gather_start(which):
        total = rs_send[which, place].astype(F32)
        if group_n - 1 <= UNROLL:
            for s in range(group_n - 1):
                scatter(which, s).wait()
                total = total + rs_recv[which, s].astype(F32)
        else:
            def add(s, value):
                scatter(which, s).wait()
                return value + rs_recv[which, s].astype(F32)

            total = lax.fori_loop(0, group_n - 1, add, total)
        ag[which, place] = total.astype(BF)
        each(group_n - 1, lambda s: gather(which, s).start())

    def pair_start(which):
        each(group_n - 1, lambda s: gather(which, s).wait())
        pairs(which).start()
        outs[which][core] = ag[which]

    weight_terms(0, ht, xg, xgm)

    edge[...] = jnp.zeros_like(edge)
    unpack(0, 4, 5, 0, 3)
    unpack(1, 4, 5, 0, 8)
    turned_edge(xt)

    for g in range(rows_n // BAND):
        low = g * BAND * cols_n
        back = conv(xg, wb, low, BAND * cols_n, cols_n).reshape(BAND, cols_n, chans)
        rows = pl.ds(1 + g * BAND, BAND)
        active = hext[rows, 16 : 16 + cols_n, :] > 0
        pext[rows, 16 : 16 + cols_n, :] = jnp.where(active, back, 0.0)

    rim_active = jnp.concatenate(
        [hext[1 : 1 + rows_n, 8:16, :], hext[1 : 1 + rows_n, 16 + cols_n : 24 + cols_n, :]],
        axis=1,
    ).reshape(rim, chans) > 0
    to_rim(pext, jnp.where(rim_active, conv(xgm, wb, 0, rim, EDGE), 0.0))
    scatter_start(0)
    side_by_side(pext, xp, xpm, True)
    weight_terms(1, xt, xp, xpm)

    side_by_side(hext, xh, xhm, False)
    scatter_start(1)
    for g in range(rows_n // BAND):
        low = g * BAND * cols_n
        block = conv(xh, w_ref, low, BAND * cols_n, cols_n)
        feat_t[:, pl.ds(low, BAND * cols_n)] = block.T.astype(BF)

    feat_t[:, cells : cells + rim] = conv(xhm, w_ref, 0, rim, EDGE).T.astype(BF)

    slot_grads = dot(feat_t[...], spread[...])
    retall[:, 0:cap] = slot_grads[:, 0:cap].astype(BF)
    returns = []
    for step in range(1, lon_n):
        ret_send[step - 1] = slot_grads[:, step * cap : (step + 1) * cap].astype(BF)
        copy = remote(
            ret_send.at[step - 1], ret_recv.at[step - 1], ret_s.at[step - 1],
            ret_r.at[step - 1], {"lon": lon_id(-step)},
        )
        copy.start()
        returns.append(copy)

    gather_start(0)
    gather_start(1)
    for step in range(1, lon_n):
        returns[step - 1].wait()
        retall[:, step * cap : (step + 1) * cap] = ret_recv[step - 1]
    home = dot(retall[...], pt[...]).T
    share = tracks // frame_n
    for f in range(frame_n):
        piece = home[f * share : (f + 1) * share, :]
        qg_own[f] = piece
        qg_send[f] = piece.astype(BF)
    qgs = []
    for step in range(1, frame_n):
        copy = remote(
            qg_send.at[frame_id(step)], qg_recv.at[step - 1], qg_s.at[step - 1],
            qg_r.at[step - 1], {"frame": frame_id(step)},
        )
        copy.start()
        qgs.append(copy)

    pair_start(0)
    pair_start(1)
    total = qg_own[frame]
    for step in range(1, frame_n):
        qgs[step - 1].wait()
        total = total + qg_recv[step - 1].astype(F32)
    query_out[...] = total
    pairs(0).wait()
    pairs(1).wait()


def expand(dims, query_ref, first_ref, second_ref, query_out, first_out, second_out):
    part, group_n, chunk = dims
    query_out[...] = query_ref[...]
    for source, out in ((first_ref, first_out), (second_ref, second_out)):
        for c in range(2):
            for p in range(group_n):
                rows = min(chunk, part - p * chunk)
                if rows > 0:
                    start = c * part + p * chunk
                    out[start : start + rows, :] = source[c, p].astype(F32)[0:rows]


def per_device(
    layer_input, hidden_saved, conv_weight, queries, corr_cotangent,
    window_rows, window_cols, owner_strip,
):
    lon_n, frame_n = lax.axis_size("lon"), lax.axis_size("frame")
    _, rows_n, cols_n, chans = hidden_saved.shape
    tracks = queries.shape[0]
    cap = tracks // 4
    slots = lon_n * cap
    part = 9 * chans // 2
    group_n = lon_n // 2 * frame_n
    chunk = -(-part // group_n)
    scale = 1.0 / math.sqrt(rows_n * cols_n * lon_n * frame_n)
    dims = (lon_n, frame_n, rows_n, cols_n, chans, tracks, cap, group_n, chunk, scale)
    share = tracks // frame_n
    vm = pltpu.VMEM
    dma = pltpu.SemaphoreType.DMA
    scratch = [
        vm((rows_n + 2, EXT, chans), F32),
        vm((rows_n + 2, EXT, chans), F32),
        vm((rows_n + 2, EXT, chans), F32),
        vm(((rows_n + 2) * cols_n, 3 * chans), BF),
        vm(((rows_n + 2) * EDGE, 3 * chans), BF),
        vm(((rows_n + 2) * cols_n, 3 * chans), BF),
        vm(((rows_n + 2) * EDGE, 3 * chans), BF),
        vm(((rows_n + 2) * cols_n, 3 * chans), BF),
        vm(((rows_n + 2) * EDGE, 3 * chans), BF),
        vm((chans, rows_n * (cols_n + EDGE)), BF),
        vm((3, 3 * chans, chans), BF),
        vm((3 * chans, rows_n * (cols_n + EDGE)), BF),
        vm((3 * chans, rows_n * (cols_n + EDGE)), BF),
        vm((rows_n * (cols_n + EDGE), slots), BF),
        vm((rows_n + 2, EDGE, chans), F32),
        vm((64, tracks), F32),
        vm((slots, tracks), BF),
        vm((slots, chans), BF),
        vm((64, slots), F32),
        vm((lon_n - 1, cap + 64, chans), BF),
        vm((lon_n - 1, cap + 64, chans), BF),
        vm((HALO * rows_n, chans), F32),
        vm((2, HALO * rows_n, chans), BF),
        vm((2, HALO * rows_n, chans), BF),
        vm((lon_n - 1, chans, cap), BF),
        vm((lon_n - 1, chans, cap), BF),
        vm((chans, slots), BF),
        vm((frame_n, share, chans), BF),
        vm((frame_n, share, chans), F32),
        vm((frame_n - 1, share, chans), BF),
        vm((2, 9 * chans, chans), F32),
        vm((2, part, chans), BF),
        vm((2, part, chans), BF),
        vm((group_n * chunk, chans), F32),
        vm((2, group_n, chunk, chans), BF),
        vm((2, group_n - 1, chunk, chans), BF),
        vm((2, group_n, chunk, chans), BF),
        dma((lon_n - 1,)), dma((lon_n - 1,)),
        dma((2,)), dma((2,)),
        dma((lon_n - 1,)), dma((lon_n - 1,)),
        dma((frame_n - 1,)), dma((frame_n - 1,)),
        dma((2,)), dma((2,)),
        dma((2, group_n - 1)), dma((2, group_n - 1)),
        dma((2, group_n - 1)), dma((2, group_n - 1)),
        dma((2,)), dma((2,)),
    ]
    spec = pl.BlockSpec(memory_space=pltpu.VMEM)
    gathered = jax.ShapeDtypeStruct((2, group_n, chunk, chans), BF)
    query_grad, first, second = pl.pallas_call(
        functools.partial(kernel, dims),
        out_shape=(jax.ShapeDtypeStruct((share, chans), F32), gathered, gathered),
        in_specs=[spec] * 8,
        out_specs=(spec,) * 3,
        scratch_shapes=scratch,
        compiler_params=pltpu.CompilerParams(
            collective_id=0, has_side_effects=True, vmem_limit_bytes=60 * 1024 * 1024
        ),
    )(
        layer_input[0], hidden_saved[0], conv_weight.reshape(3, 3 * chans, chans), queries,
        corr_cotangent[0], window_rows, window_cols, owner_strip[:, :, 0],
    )
    weight = jax.ShapeDtypeStruct((9 * chans, chans), F32)
    query_grad, first, second = pl.pallas_call(
        functools.partial(expand, (part, group_n, chunk)),
        out_shape=(jax.ShapeDtypeStruct((share, chans), F32), weight, weight),
        in_specs=[spec] * 3,
        out_specs=(spec,) * 3,
    )(query_grad, first, second)
    return (
        query_grad,
        first.reshape(3, 3, chans, chans),
        second.reshape(3, 3, chans, chans),
    )


def solution(mesh):
    placed = (
        P("frame", None, "lon", None),
        P("frame", None, "lon", None),
        P(),
        P("lon", None),
        P("frame", None, "lon"),
        P("frame", "lon"),
        P("frame", "lon"),
        P("frame", "lon", None),
    )
    return jax.shard_map(
        per_device,
        mesh=mesh,
        in_specs=placed,
        out_specs=(P(("lon", "frame"), None), P(), P()),
        check_vma=False,
    )
```

```python
import functools
import math

import jax
import jax.numpy as jnp
from jax import lax
from jax.experimental import pallas as pl
from jax.experimental.pallas import tpu as pltpu
from jax.sharding import PartitionSpec as P

WIN = 7
EDGE = 16
EXT = 160
BF = jnp.bfloat16
F32 = jnp.float32
MESH = pl.DeviceIdType.MESH
HALO = 9
BAND = 4
UNROLL = 32


def dot(a, b):
    return jnp.dot(a, b, preferred_element_type=F32)


def each(count, body):
    if count <= UNROLL:
        for s in range(count):
            body(s)
    else:
        pl.loop(0, count)(body)


def kernel(
    dims,
    x_ref, h_ref, w_ref, q_ref, cot_ref, rows_ref, cols_ref, own_ref,
    query_out, first_out, second_out,
    hext, gext, pext, xh, xhm, xg, xgm, xp, xpm, feat_t, wb, ht, xt, spread, edge,
    cm, pt, qall, cmall,
    pay_send, pay_recv, strip, halo_send, halo_recv,
    ret_send, ret_recv, retall, qg_send, qg_own, qg_recv,
    grads, half_send, half_recv, acc, rs_send, rs_recv, ag,
    pay_s, pay_r, halo_s, halo_r, ret_s, ret_r, qg_s, qg_r,
    half_s, half_r, rs_s, rs_r, ag_s, ag_r, pair_s, pair_r,
):
    lon_n, frame_n, rows_n, cols_n, chans, tracks, cap, group_n, chunk, scale = dims
    lon, frame = lax.axis_index("lon"), lax.axis_index("frame")
    slots = lon_n * cap
    half = rows_n // 2
    core = lax.rem(lon, 2)
    place = (lon // 2) * frame_n + frame
    part = 9 * chans // 2

    def lon_id(steps):
        return lax.rem(lon + steps + lon_n, lon_n)

    def frame_id(steps):
        return lax.rem(frame + steps + frame_n, frame_n)

    def group_id(steps):
        chip = lax.rem(lon // 2 + steps % (lon_n // 2), lon_n // 2)
        return chip * frame_n + lax.rem(frame + steps // (lon_n // 2), frame_n)

    def group_device(p):
        return {"lon": (p // frame_n) * 2 + core, "frame": lax.rem(p, frame_n)}

    pair = {"lon": lon + 1 - 2 * core}

    def remote(src, dst, send, recv, where):
        return pltpu.make_async_remote_copy(
            src_ref=src, dst_ref=dst, send_sem=send, recv_sem=recv,
            device_id=where, device_id_type=MESH,
        )

    barrier = pltpu.get_barrier_semaphore()
    for step in range(1, lon_n):
        pl.semaphore_signal(barrier, inc=1, device_id={"lon": lon_id(step)}, device_id_type=MESH)

    def greet(s):
        pl.semaphore_signal(
            barrier, inc=1, device_id=group_device(group_id(s + 1)), device_id_type=MESH
        )

    each(group_n - 1, greet)

    for side in range(2):
        first = cols_n - 8 if side == 0 else 0
        h_edge = h_ref[:, first : first + 8].astype(F32)
        x_edge = x_ref[:, first : first + 8].astype(F32)
        for r in range(rows_n):
            if side == 0:
                strip[HALO * r : HALO * r + 4, :] = h_edge[r, 4:8]
                strip[HALO * r + 4 : HALO * r + 9, :] = x_edge[r, 3:8]
            else:
                strip[HALO * r : HALO * r + 4, :] = h_edge[r, 0:4]
                strip[HALO * r + 4 : HALO * r + 9, :] = x_edge[r, 0:5]
        halo_send[side] = strip[...].astype(BF)

    owners = own_ref[...]
    marks = (owners == lax.broadcasted_iota(jnp.int32, (16, tracks), 0)).astype(F32)
    earlier = (
        lax.broadcasted_iota(jnp.int32, (tracks, tracks), 0)
        < lax.broadcasted_iota(jnp.int32, (tracks, tracks), 1)
    ).astype(F32).astype(BF)
    before = dot(marks.astype(BF), earlier)
    rank = jnp.sum(before * marks, axis=0, keepdims=True).astype(jnp.int32)
    slot = owners * cap + rank
    cm[...] = jnp.zeros_like(cm)
    for i in range(WIN):
        cm[8 * i : 8 * i + WIN, :] = cot_ref[WIN * i : WIN * i + WIN, :].astype(F32)
    cm[56:57, :] = rows_ref[...].astype(F32)
    cm[57:58, :] = (cols_ref[...] + 3).astype(F32)
    cm_half = cm[...].astype(BF)

    pays = []
    for step in list(range(1, lon_n)) + [0]:
        local = slot - lon_id(step) * cap
        hot = (local == lax.broadcasted_iota(jnp.int32, (cap, tracks), 0)).astype(F32).astype(BF)
        pt[step * cap : (step + 1) * cap, :] = hot
        q_part = dot(hot, q_ref[...]).astype(BF)
        c_part = lax.dot_general(
            cm_half, hot, (((1,), (1,)), ((), ())), preferred_element_type=F32
        )
        if step:
            pay_send[step - 1, 0:cap, :] = q_part
            pay_send[step - 1, cap : cap + 64, :] = c_part.astype(BF)
        else:
            qall[0:cap, :] = q_part
            cmall[:, 0:cap] = c_part

    pl.semaphore_wait(barrier, lon_n - 1 + group_n - 1)
    for step in range(1, lon_n):
        copy = remote(
            pay_send.at[step - 1], pay_recv.at[step - 1], pay_s.at[step - 1],
            pay_r.at[step - 1], {"lon": lon_id(step)},
        )
        copy.start()
        pays.append(copy)
    halos = [
        remote(halo_send.at[0], halo_recv.at[0], halo_s.at[0], halo_r.at[0], {"lon": lon_id(1)}),
        remote(halo_send.at[1], halo_recv.at[1], halo_s.at[1], halo_r.at[1], {"lon": lon_id(-1)}),
    ]
    for copy in halos:
        copy.start()

    for a in range(3):
        for b in range(3):
            tap = w_ref[2 - a, b * chans : (b + 1) * chans, :].astype(F32)
            wb[a, b * chans : (b + 1) * chans, :] = tap.T.astype(BF)

    cells, rim = rows_n * cols_n, rows_n * EDGE

    def turned(src, out):
        out[0:chans, 0:cols_n] = jnp.zeros((chans, cols_n), BF)
        out[2 * chans : 3 * chans, cells - cols_n : cells] = jnp.zeros((chans, cols_n), BF)
        for r in range(rows_n):
            tile = src[r].astype(F32).T.astype(BF)
            for a in range(3):
                if 0 <= r + 1 - a < rows_n:
                    at = (r + 1 - a) * cols_n
                    out[a * chans : (a + 1) * chans, at : at + cols_n] = tile

    def turned_edge(out):
        for a in range(3):
            block = edge[a : a + rows_n].reshape(rim, chans)
            out[a * chans : (a + 1) * chans, cells : cells + rim] = block.T.astype(BF)

    def side_by_side(ext, out, out_edge, flip):
        for r in range(1, rows_n + 1):
            at, low = r * cols_n, r * EDGE
            for b in range(3):
                by = 1 - b if flip else b - 1
                lanes = slice(b * chans, (b + 1) * chans)
                out[pl.ds(at, cols_n), lanes] = ext[r, 16 + by : 16 + by + cols_n, :].astype(BF)
                rim_cells = jnp.concatenate(
                    [
                        ext[r, 8 + by : 16 + by, :],
                        ext[r, 16 + cols_n + by : 24 + cols_n + by, :],
                    ],
                    axis=0,
                )
                out_edge[pl.ds(low, EDGE), lanes] = rim_cells.astype(BF)

    def conv(source, weight, start, count, step):
        total = None
        for a in range(3):
            term = dot(source[pl.ds(start + a * step, count), :], weight[a])
            total = term if total is None else total + term
        return total

    def spread_block(step):
        lanes = slice(step * cap, (step + 1) * cap)
        rows_t = cmall[56:57, lanes].astype(jnp.int32)
        cols_t = cmall[57:58, lanes].astype(jnp.int32) - 3
        placed = []
        for r in range(rows_n):
            value = jnp.zeros((8, cap), F32)
            for i in range(WIN):
                if 0 <= r - i <= rows_n - WIN:
                    value = jnp.where(rows_t == r - i, cmall[8 * i : 8 * i + 8, lanes], value)
            placed.append(value)

        def tiles(column, base, stride):
            offset = column - cols_t
            hits = [offset == j for j in range(WIN)]
            for r in range(rows_n):
                value = jnp.zeros((16, cap), F32)
                for j in range(WIN):
                    value = jnp.where(hits[j], placed[r][j : j + 1, :], value)
                start = pl.multiple_of(r * stride + base, 16)
                spread[pl.ds(start, 16), lanes] = value.astype(BF)

        count = lax.broadcasted_iota(jnp.int32, (16, cap), 0)

        @pl.loop(0, cols_n // 16)
        def _(tile):
            tiles(count + tile * 16, tile * 16, cols_n)

        tiles(jnp.where(count < 8, count - 8, count + (cols_n - 8)), cells, EDGE)

    hext[...] = jnp.zeros_like(hext)
    gext[...] = jnp.zeros_like(gext)
    pext[...] = jnp.zeros_like(pext)

    @pl.loop(0, rows_n)
    def _(r):
        hext[r + 1, 16 : 16 + cols_n, :] = h_ref[r].astype(F32)

    for wide in (xh, xg, xp):
        wide[0:cols_n, :] = jnp.zeros((cols_n, 3 * chans), BF)
        wide[cells + cols_n :, :] = jnp.zeros((cols_n, 3 * chans), BF)
    for thin in (xhm, xgm, xpm):
        thin[0:EDGE, :] = jnp.zeros((EDGE, 3 * chans), BF)
        thin[rim + EDGE :, :] = jnp.zeros((EDGE, 3 * chans), BF)

    turned(h_ref, ht)
    turned(x_ref, xt)
    spread_block(0)

    for step in range(1, lon_n):
        pays[step - 1].wait()
        qall[step * cap : (step + 1) * cap, :] = pay_recv[step - 1, 0:cap, :]
        cmall[:, step * cap : (step + 1) * cap] = pay_recv[step - 1, cap : cap + 64, :].astype(F32)
        spread_block(step)

    def to_rim(ext, block):
        block = block.reshape(rows_n, EDGE, chans)
        ext[1 : 1 + rows_n, 8:16, :] = block[:, 0:8]
        ext[1 : 1 + rows_n, 16 + cols_n : 24 + cols_n, :] = block[:, 8:16]

    for g in range(rows_n // BAND):
        low = g * BAND * cols_n
        block = dot(spread[pl.ds(low, BAND * cols_n), :], qall[...])
        gext[pl.ds(1 + g * BAND, BAND), 16 : 16 + cols_n, :] = block.reshape(BAND, cols_n, chans)

    to_rim(gext, dot(spread[cells : cells + rim, :], qall[...]))
    for copy in halos:
        copy.wait()

    def unpack(side, first, count, out_at, in_edge):
        strip[...] = halo_recv[side].astype(F32)
        for r in range(rows_n):
            at = HALO * r + first
            edge[r + 1, in_edge : in_edge + count, :] = strip[at : at + count, :]
            if out_at:
                hext[r + 1, out_at : out_at + count, :] = strip[at : at + count, :]

    edge[...] = jnp.zeros_like(edge)
    unpack(0, 0, 4, 12, 4)
    unpack(1, 0, 4, 16 + cols_n, 8)
    turned_edge(ht)
    side_by_side(gext, xg, xgm, True)

    def halves(which):
        return remote(
            half_send.at[which], half_recv.at[which], half_s.at[which], half_r.at[which], pair
        )

    def scatter(which, s):
        p = group_id(s + 1)
        return remote(
            rs_send.at[which, p], rs_recv.at[which, s], rs_s.at[which, s], rs_r.at[which, s],
            group_device(p),
        )

    def gather(which, s):
        return remote(
            ag.at[which, place], ag.at[which, place], ag_s.at[which, s], ag_r.at[which, s],
            group_device(group_id(s + 1)),
        )

    outs = (second_out, first_out)

    def pairs(which):
        return remote(
            ag.at[which], outs[which].at[core], pair_s.at[which], pair_r.at[which], pair
        )

    def weight_terms(which, turned_source, grad, grad_edge):
        term = dot(turned_source[:, 0:cells], grad[cols_n : cols_n + cells, :])
        term = term + dot(turned_source[:, cells : cells + rim], grad_edge[EDGE : EDGE + rim, :])
        term = term * scale
        for a in range(3):
            for b in range(3):
                row = (3 * a + b) * chans
                grads[which, row : row + chans, :] = term[
                    a * chans : (a + 1) * chans, b * chans : (b + 1) * chans
                ]
        other = pl.ds(pl.multiple_of((1 - core) * part, 8), part)
        half_send[which] = grads[which, other, :].astype(BF)
        halves(which).start()

    def scatter_start(which):
        halves(which).wait()
        mine = pl.ds(pl.multiple_of(core * part, 8), part)
        if group_n * chunk > part:
            acc[part:, :] = jnp.zeros((group_n * chunk - part, chans), F32)
        acc[0:part, :] = grads[which, mine, :] + half_recv[which].astype(F32)
        for p in range(group_n):
            rs_send[which, p] = acc[p * chunk : (p + 1) * chunk, :].astype(BF)
        each(group_n - 1, lambda s: scatter(which, s).start())

    def gather_start(which):
        total = rs_send[which, place].astype(F32)
        if group_n - 1 <= UNROLL:
            for s in range(group_n - 1):
                scatter(which, s).wait()
                total = total + rs_recv[which, s].astype(F32)
        else:
            def add(s, value):
                scatter(which, s).wait()
                return value + rs_recv[which, s].astype(F32)

            total = lax.fori_loop(0, group_n - 1, add, total)
        ag[which, place] = total.astype(BF)
        each(group_n - 1, lambda s: gather(which, s).start())

    def pair_start(which):
        each(group_n - 1, lambda s: gather(which, s).wait())
        pairs(which).start()
        outs[which][core] = ag[which]

    weight_terms(0, ht, xg, xgm)

    edge[...] = jnp.zeros_like(edge)
    unpack(0, 4, 5, 0, 3)
    unpack(1, 4, 5, 0, 8)
    turned_edge(xt)

    for g in range(rows_n // BAND):
        low = g * BAND * cols_n
        back = conv(xg, wb, low, BAND * cols_n, cols_n).reshape(BAND, cols_n, chans)
        rows = pl.ds(1 + g * BAND, BAND)
        active = hext[rows, 16 : 16 + cols_n, :] > 0
        pext[rows, 16 : 16 + cols_n, :] = jnp.where(active, back, 0.0)

    rim_active = jnp.concatenate(
        [hext[1 : 1 + rows_n, 8:16, :], hext[1 : 1 + rows_n, 16 + cols_n : 24 + cols_n, :]],
        axis=1,
    ).reshape(rim, chans) > 0
    to_rim(pext, jnp.where(rim_active, conv(xgm, wb, 0, rim, EDGE), 0.0))
    scatter_start(0)
    side_by_side(pext, xp, xpm, True)
    weight_terms(1, xt, xp, xpm)

    side_by_side(hext, xh, xhm, False)
    scatter_start(1)
    for g in range(rows_n // BAND):
        low = g * BAND * cols_n
        block = conv(xh, w_ref, low, BAND * cols_n, cols_n)
        feat_t[:, pl.ds(low, BAND * cols_n)] = block.T.astype(BF)

    feat_t[:, cells : cells + rim] = conv(xhm, w_ref, 0, rim, EDGE).T.astype(BF)

    slot_grads = dot(feat_t[...], spread[...])
    retall[:, 0:cap] = slot_grads[:, 0:cap].astype(BF)
    returns = []
    for step in range(1, lon_n):
        ret_send[step - 1] = slot_grads[:, step * cap : (step + 1) * cap].astype(BF)
        copy = remote(
            ret_send.at[step - 1], ret_recv.at[step - 1], ret_s.at[step - 1],
            ret_r.at[step - 1], {"lon": lon_id(-step)},
        )
        copy.start()
        returns.append(copy)

    gather_start(0)
    gather_start(1)
    for step in range(1, lon_n):
        returns[step - 1].wait()
        retall[:, step * cap : (step + 1) * cap] = ret_recv[step - 1]
    home = dot(retall[...], pt[...]).T
    share = tracks // frame_n
    for f in range(frame_n):
        piece = home[f * share : (f + 1) * share, :]
        qg_own[f] = piece
        qg_send[f] = piece.astype(BF)
    qgs = []
    for step in range(1, frame_n):
        copy = remote(
            qg_send.at[frame_id(step)], qg_recv.at[step - 1], qg_s.at[step - 1],
            qg_r.at[step - 1], {"frame": frame_id(step)},
        )
        copy.start()
        qgs.append(copy)

    pair_start(0)
    pair_start(1)
    total = qg_own[frame]
    for step in range(1, frame_n):
        qgs[step - 1].wait()
        total = total + qg_recv[step - 1].astype(F32)
    query_out[...] = total
    pairs(0).wait()
    pairs(1).wait()


def expand(dims, query_ref, first_ref, second_ref, query_out, first_out, second_out):
    part, group_n, chunk = dims
    query_out[...] = query_ref[...]
    for source, out in ((first_ref, first_out), (second_ref, second_out)):
        for c in range(2):
            for p in range(group_n):
                rows = min(chunk, part - p * chunk)
                if rows > 0:
                    start = c * part + p * chunk
                    out[start : start + rows, :] = source[c, p].astype(F32)[0:rows]


def per_device(
    layer_input, hidden_saved, conv_weight, queries, corr_cotangent,
    window_rows, window_cols, owner_strip,
):
    lon_n, frame_n = lax.axis_size("lon"), lax.axis_size("frame")
    _, rows_n, cols_n, chans = hidden_saved.shape
    tracks = queries.shape[0]
    cap = tracks // 4
    slots = lon_n * cap
    part = 9 * chans // 2
    group_n = lon_n // 2 * frame_n
    chunk = -(-part // group_n)
    scale = 1.0 / math.sqrt(rows_n * cols_n * lon_n * frame_n)
    dims = (lon_n, frame_n, rows_n, cols_n, chans, tracks, cap, group_n, chunk, scale)
    share = tracks // frame_n
    vm = pltpu.VMEM
    dma = pltpu.SemaphoreType.DMA
    scratch = [
        vm((rows_n + 2, EXT, chans), F32),
        vm((rows_n + 2, EXT, chans), F32),
        vm((rows_n + 2, EXT, chans), F32),
        vm(((rows_n + 2) * cols_n, 3 * chans), BF),
        vm(((rows_n + 2) * EDGE, 3 * chans), BF),
        vm(((rows_n + 2) * cols_n, 3 * chans), BF),
        vm(((rows_n + 2) * EDGE, 3 * chans), BF),
        vm(((rows_n + 2) * cols_n, 3 * chans), BF),
        vm(((rows_n + 2) * EDGE, 3 * chans), BF),
        vm((chans, rows_n * (cols_n + EDGE)), BF),
        vm((3, 3 * chans, chans), BF),
        vm((3 * chans, rows_n * (cols_n + EDGE)), BF),
        vm((3 * chans, rows_n * (cols_n + EDGE)), BF),
        vm((rows_n * (cols_n + EDGE), slots), BF),
        vm((rows_n + 2, EDGE, chans), F32),
        vm((64, tracks), F32),
        vm((slots, tracks), BF),
        vm((slots, chans), BF),
        vm((64, slots), F32),
        vm((lon_n - 1, cap + 64, chans), BF),
        vm((lon_n - 1, cap + 64, chans), BF),
        vm((HALO * rows_n, chans), F32),
        vm((2, HALO * rows_n, chans), BF),
        vm((2, HALO * rows_n, chans), BF),
        vm((lon_n - 1, chans, cap), BF),
        vm((lon_n - 1, chans, cap), BF),
        vm((chans, slots), BF),
        vm((frame_n, share, chans), BF),
        vm((frame_n, share, chans), F32),
        vm((frame_n - 1, share, chans), BF),
        vm((2, 9 * chans, chans), F32),
        vm((2, part, chans), BF),
        vm((2, part, chans), BF),
        vm((group_n * chunk, chans), F32),
        vm((2, group_n, chunk, chans), BF),
        vm((2, group_n - 1, chunk, chans), BF),
        vm((2, group_n, chunk, chans), BF),
        dma((lon_n - 1,)), dma((lon_n - 1,)),
        dma((2,)), dma((2,)),
        dma((lon_n - 1,)), dma((lon_n - 1,)),
        dma((frame_n - 1,)), dma((frame_n - 1,)),
        dma((2,)), dma((2,)),
        dma((2, group_n - 1)), dma((2, group_n - 1)),
        dma((2, group_n - 1)), dma((2, group_n - 1)),
        dma((2,)), dma((2,)),
    ]
    spec = pl.BlockSpec(memory_space=pltpu.VMEM)
    gathered = jax.ShapeDtypeStruct((2, group_n, chunk, chans), BF)
    query_grad, first, second = pl.pallas_call(
        functools.partial(kernel, dims),
        out_shape=(jax.ShapeDtypeStruct((share, chans), F32), gathered, gathered),
        in_specs=[spec] * 8,
        out_specs=(spec,) * 3,
        scratch_shapes=scratch,
        compiler_params=pltpu.CompilerParams(
            collective_id=0, has_side_effects=True, vmem_limit_bytes=60 * 1024 * 1024
        ),
    )(
        layer_input[0], hidden_saved[0], conv_weight.reshape(3, 3 * chans, chans), queries,
        corr_cotangent[0], window_rows, window_cols, owner_strip[:, :, 0],
    )
    weight = jax.ShapeDtypeStruct((9 * chans, chans), F32)
    query_grad, first, second = pl.pallas_call(
        functools.partial(expand, (part, group_n, chunk)),
        out_shape=(jax.ShapeDtypeStruct((share, chans), F32), weight, weight),
        in_specs=[spec] * 3,
        out_specs=(spec,) * 3,
    )(query_grad, first, second)
    return (
        query_grad,
        first.reshape(3, 3, chans, chans),
        second.reshape(3, 3, chans, chans),
    )


def solution(mesh):
    placed = (
        P("frame", None, "lon", None),
        P("frame", None, "lon", None),
        P(),
        P("lon", None),
        P("frame", None, "lon"),
        P("frame", "lon"),
        P("frame", "lon"),
        P("frame", "lon", None),
    )
    return jax.shard_map(
        per_device,
        mesh=mesh,
        in_specs=placed,
        out_specs=(P(("lon", "frame"), None), P(), P()),
        check_vma=False,
    )
```
